1024 devices in a mesh: sx: 32 (over x, z_hi, core), sy: 32 (over y, z_lo).
Axes of the slice: x: 8, y: 8, z: 8 (z_hi: 2, z_lo: 4; z = z_hi * 4 + z_lo), core: 2. Of those that a mesh axis runs over, the one named last changes fastest.
Arguments:
- residual: float32 [1536, 1536, 128], P('sx', 'sy'), may hold values from -6 to 6
- labels: int32 [1536, 1536], P('sx', 'sy'), may hold values from 0 to 7
- region_kappa: float32 [8], replicated, may hold values from 1 to 16
- coarse_basis: float32 [8, 1536, 1536], P(None, 'sx', 'sy'), may hold values from -0.5 to 0.5
- primal_cells: int32 [32, 32, 8], P('sx', 'sy'), may hold values from 0 to 2303
- level_two: float32 [32, 256, 256], P('sx', 'sy'), may hold values from -12 to 12
- row_restrict: float32 [32, 256, 16], P('sx', 'sy'), may hold values from -0.375 to 0.375
- level_three: float32 [512, 512], P('sx'), may hold values from -12 to 12
- row_order: int32 [512], replicated, may hold values from 0 to 511, each once
Outputs:
- result: float32 [1536, 1536, 128], P('sx', 'sy')
The draws below stay inside these ranges and needn't reach their ends.
Inputs may be any that keep to these rules, and one draw needn't show every extreme that they name: `primal_cells`: entry k of subdomain (i, j) is a cell index, row-major within that subdomain's 48 x 48 cells.
All inputs are finite; a program needn't handle non-finite values.
Results may differ from the reference program's by a relative error of at most 0.00012.
Values sent between devices are 32-bit elements; how exact they have to be, the bound alone decides.
No kernel may reach another device: no remote copies, remote signals or barrier semaphores. Data moves between devices by JAX's collectives and lax.ppermute only.
A program may use at most 32 MiB of HBM per device.

```python
import math
import jax
import jax.numpy as jnp
from jax import lax

CX = 48
CY = 48
NRHS = 128
CHEB = 6
NC = 8
NC3 = 16
REGIONS = 8
NX = 1536
NY = 1536
N_SX = 32
N_SY = 32


def dominant_matrix(key, count_outer, order_size):
    noise_key = jax.random.fold_in(key, 11)
    noise_part = jax.random.normal(noise_key, (count_outer, order_size, order_size), jnp.float32)
    identity = jnp.eye(order_size, dtype=jnp.float32)
    return identity + 0.6 / math.sqrt(order_size) * noise_part


def draw_level_two(key, part):
    return dominant_matrix(key, N_SX, N_SY * NC)


def draw_level_three(key, part):
    return dominant_matrix(key, 1, N_SX * NC3)[0]


def plant(entries, stream_key, smallest, largest):
    longest = entries.shape.index(max(entries.shape))
    spots = []
    for shift in (0, 1):
        where = [jax.random.randint(jax.random.fold_in(stream_key, axis), (), 0, length) for axis, length in enumerate(entries.shape)]
        where[longest] = (where[longest] + shift) % entries.shape[longest]
        spots.append(tuple(where))
    return entries.at[spots[0]].set(smallest).at[spots[1]].set(largest)


def steps_of(own_key, shape, pieces, low, largest):
    loudness, own = 1.0, jax.random.fold_in(own_key, 6)
    for dim, parts in pieces:
        draws = jnp.exp(jax.random.uniform(jax.random.fold_in(own, dim), (parts,), jnp.float32, low / len(pieces), largest / len(pieces)))
        loudness = loudness * jnp.repeat(draws, shape[dim] // parts).reshape([-1 if axis == dim else 1 for axis in range(len(shape))])
    return loudness


def bell_draw(rng, shape, width, bound, cuts=(), kind=jnp.bfloat16):
    values = jax.random.normal(rng, shape, jnp.float32) * width
    if len(cuts) > 0:
        values = steps_of(rng, shape, cuts, -0.22, 0.18) * values
    return jnp.clip(values, min=-bound, max=bound).astype(kind)


def setup_inputs(seed: int = 0) -> dict:
    keys = jax.random.split(jax.random.key(seed), 10)
    return {
        "residual": bell_draw(keys[0], (NX, NY, NRHS), 1.0, 6.0, ((0, 32), (1, 32)), jnp.float32),
        "labels": plant(jax.random.randint(keys[1], (NX, NY), 0, REGIONS), jax.random.fold_in(keys[1], 1), 0, REGIONS - 1).astype(jnp.int32),
        "region_kappa": jnp.clip(jnp.exp(jax.random.uniform(keys[2], (REGIONS,), jnp.float32, math.log(1.0), math.log(16.0))), 1.0, 16.0),
        "coarse_basis": bell_draw(keys[3], (NC, NX, NY), 0.08, 0.5, ((1, 32), (2, 32)), jnp.float32),
        "primal_cells": plant(jax.random.randint(keys[4], (N_SX, N_SY, NC), 0, CX * CY), jax.random.fold_in(keys[4], 1), 0, (CX * CY) - 1).astype(jnp.int32),
        "level_two": draw_level_two(jax.random.fold_in(keys[9], 71), 0),
        "row_restrict": bell_draw(keys[6], (N_SX, N_SY * NC, NC3), (N_SY * NC) ** -0.5, 0.375, ((0, 32), (1, 32)), jnp.float32),
        "level_three": draw_level_three(jax.random.fold_in(keys[9], 71), 0),
        "row_order": jax.random.permutation(keys[8], N_SX * NC3).astype(jnp.int32),
    }


shift_mass = 1.0
lower_edge = 1.0
upper_edge = 144.0
highest = lax.Precision.HIGHEST

def stencil_blocks(values_in):
    padded = jnp.pad(values_in, ((0, 0), (1, 1), (0, 0), (1, 1), (0, 0)))
    beside = padded[:, 2:, :, 1:-1] + padded[:, :-2, :, 1:-1] + padded[:, 1:-1, :, 2:] + padded[:, 1:-1, :, :-2]
    return (4.0 + shift_mass) * values_in - beside

def stencil_whole(values_in):
    padded = jnp.pad(values_in, ((1, 1), (1, 1), (0, 0)))
    beside = padded[2:, 1:-1] + padded[:-2, 1:-1] + padded[1:-1, 2:] + padded[1:-1, :-2]
    return (4.0 + shift_mass) * values_in - beside

def chebyshev(rhs_field, apply_op):
    centre = 0.5 * (upper_edge + lower_edge)
    half_range = 0.5 * (upper_edge - lower_edge)
    sigma_ratio = centre / half_range
    rho_now = 1.0 / sigma_ratio
    direction = rhs_field / centre
    solution = direction
    remainder = rhs_field
    for sweep_index in range(CHEB):
        remainder = remainder - apply_op(direction)
        rho_next = 1.0 / (2.0 * sigma_ratio - rho_now)
        direction = rho_next * rho_now * direction + 2.0 * rho_next / half_range * remainder
        solution = solution + direction
        rho_now = rho_next
    return solution

def reference(residual, labels, region_kappa, coarse_basis, primal_cells, level_two, row_restrict, level_three, row_order):
    onehot = (labels[..., None] == jnp.arange(REGIONS, dtype=jnp.int32)).astype(jnp.float32)
    root_coef = jnp.sqrt(lax.optimization_barrier(jnp.sum(onehot * region_kappa, axis=-1)))[..., None]
    root_blocks = root_coef.reshape(N_SX, CX, N_SY, CY, 1)
    basis_cells = coarse_basis.reshape(NC, N_SX, CX, N_SY, CY).transpose(1, 3, 0, 2, 4).reshape(N_SX, N_SY, NC, CX * CY)
    primal = primal_cells.astype(jnp.int32)
    order_table = (row_order[:, None] == jnp.arange(N_SX * NC3, dtype=jnp.int32)[None, :]).astype(jnp.float32)
    restrict_cells = row_restrict.reshape(N_SX, N_SY, NC, NC3)
    block_cols = 16 if NRHS % 16 == 0 else NRHS
    block_count = NRHS // block_cols

    def apply_local(values_in):
        return root_blocks * stencil_blocks(root_blocks * values_in)

    def to_cells(values_in):
        return values_in.reshape(N_SX, CX, N_SY, CY, block_cols).transpose(0, 2, 1, 3, 4).reshape(N_SX, N_SY, CX * CY, block_cols)

    def solve_block(resid_block):
        z_first = chebyshev(resid_block.reshape(N_SX, CX, N_SY, CY, block_cols), apply_local).reshape(NX, NY, block_cols)
        slack_field = resid_block - root_coef * stencil_whole(root_coef * z_first)
        slack_cells = to_cells(slack_field)
        picked = jnp.take_along_axis(slack_cells, jnp.broadcast_to(primal[..., None], (N_SX, N_SY, NC, block_cols)), axis=2)
        coarse_res = jnp.einsum('xykc,xycj->xykj', basis_cells, slack_cells, precision=highest) + picked
        row_values = coarse_res.reshape(N_SX, N_SY * NC, block_cols)
        coarse_two = jnp.einsum('xmn,xnj->xmj', level_two, row_values, precision=highest).reshape(N_SX, N_SY, NC, block_cols)
        row_terms = jnp.einsum('xnl,xnj->xlj', row_restrict, row_values, precision=highest).reshape(N_SX * NC3, block_cols)
        placed = jnp.einsum('ij,ib->jb', order_table, row_terms, precision=highest)
        coarse_three = jnp.dot(level_three, placed, precision=highest).reshape(N_SX, NC3, block_cols)
        coarse = coarse_two + jnp.einsum('xykl,xlj->xykj', restrict_cells, coarse_three, precision=highest)
        result_cells = to_cells(z_first) + jnp.einsum('xykc,xykj->xycj', basis_cells, coarse, precision=highest)
        return result_cells.reshape(N_SX, N_SY, CX, CY, block_cols).transpose(0, 2, 1, 3, 4).reshape(NX, NY, block_cols)
    stacked = residual.reshape(NX, NY, block_count, block_cols).transpose(2, 0, 1, 3)
    results = lax.map(solve_block, stacked)
    return results.transpose(1, 2, 0, 3).reshape(NX, NY, NRHS)
```

```python
import jax
import jax.numpy as jnp
from jax import lax
from jax.sharding import PartitionSpec as P

CHEB = 6


shift_mass = 1.0
lower_edge = 1.0
upper_edge = 144.0
highest = lax.Precision.HIGHEST


def neighbour_edges(block, axis, dim):
    count = lax.axis_size(axis)
    forward = [(i, i + 1) for i in range(count - 1)]
    backward = [(target, source) for source, target in forward]
    low = lax.ppermute(lax.slice_in_dim(block, block.shape[dim] - 1, None, axis=dim), axis, forward)
    high = lax.ppermute(lax.slice_in_dim(block, 0, 1, axis=dim), axis, backward)
    return low, high


def gathered(block, axis):
    count = lax.axis_size(axis)
    copies = jnp.broadcast_to(block[None], (count,) + block.shape)
    return lax.all_to_all(copies, axis, 0, 0, tiled=True)


def stencil(padded, values_in):
    beside = padded[2:, 1:-1] + padded[:-2, 1:-1] + padded[1:-1, 2:] + padded[1:-1, :-2]
    return (4.0 + shift_mass) * values_in - beside


def chebyshev(rhs_field, apply_op):
    centre = 0.5 * (upper_edge + lower_edge)
    half_range = 0.5 * (upper_edge - lower_edge)
    sigma_ratio = centre / half_range
    rho_now = 1.0 / sigma_ratio
    direction = rhs_field / centre
    solution = direction
    remainder = rhs_field
    for sweep_index in range(CHEB):
        remainder = remainder - apply_op(direction)
        rho_next = 1.0 / (2.0 * sigma_ratio - rho_now)
        direction = rho_next * rho_now * direction + 2.0 * rho_next / half_range * remainder
        solution = solution + direction
        rho_now = rho_next
    return solution


def shards(
    residual,
    labels,
    region_kappa,
    coarse_basis,
    primal_cells,
    level_two,
    row_restrict,
    level_three,
    row_order,
):
    cells_x, cells_y, rhs_count = residual.shape
    coarse_count = coarse_basis.shape[0]
    onehot = (labels[..., None] == jnp.arange(region_kappa.shape[0], dtype=jnp.int32)).astype(
        jnp.float32
    )
    root_coef = jnp.sqrt(jnp.sum(onehot * region_kappa, axis=-1))[..., None]

    def apply_local(values_in):
        scaled_in = root_coef * values_in
        return root_coef * stencil(jnp.pad(scaled_in, ((1, 1), (1, 1), (0, 0))), scaled_in)

    z_first = chebyshev(residual, apply_local)
    scaled = root_coef * z_first
    row_low, row_high = neighbour_edges(scaled, "sx", 0)
    col_low, col_high = neighbour_edges(scaled, "sy", 1)
    tall = jnp.concatenate([row_low, scaled, row_high], axis=0)
    padded = jnp.concatenate(
        [jnp.pad(col_low, ((1, 1), (0, 0), (0, 0))), tall, jnp.pad(col_high, ((1, 1), (0, 0), (0, 0)))], axis=1
    )
    slack_field = residual - root_coef * stencil(padded, scaled)
    cell_count = cells_x * cells_y
    slack_cells = slack_field.reshape(cell_count, rhs_count)
    basis_cells = coarse_basis.reshape(coarse_count, cell_count)
    picked = jnp.take(slack_cells, primal_cells.reshape(-1), axis=0)
    coarse_res = jnp.dot(basis_cells, slack_cells, precision=highest) + picked
    local_two = level_two[0]
    local_restrict = row_restrict[0]
    partial_value = lax.dot_general(
        local_restrict, coarse_res, (((0,), (0,)), ((), ())), precision=highest
    )
    everyone = gathered(jnp.concatenate([coarse_res, partial_value], axis=0), "sy")
    row_values = everyone[:, :coarse_count].reshape(-1, rhs_count)
    row_terms = jnp.sum(everyone[:, coarse_count:], axis=0)
    coarse_two = jnp.dot(local_two, row_values, precision=highest)
    order_table = (
        row_order[None, :] == jnp.arange(row_order.shape[0], dtype=jnp.int32)[:, None]
    ).astype(jnp.float32)
    picked_cols = jnp.dot(level_three, order_table, precision=highest)
    shard_piece = gathered(row_terms, "sx").reshape(-1, rhs_count)
    coarse_three = jnp.dot(picked_cols, shard_piece, precision=highest)
    coarse = coarse_two + jnp.dot(local_restrict, coarse_three, precision=highest)
    correction = lax.dot_general(basis_cells, coarse, (((0,), (0,)), ((), ())), precision=highest)
    return z_first + correction.reshape(cells_x, cells_y, rhs_count)


def solution(mesh):
    in_specs = (
        P("sx", "sy", None),
        P("sx", "sy"),
        P(),
        P(None, "sx", "sy"),
        P("sx", "sy", None),
        P("sx", "sy", None),
        P("sx", "sy", None),
        P("sx", None),
        P(),
    )
    out_specs = P("sx", "sy", None)
    return jax.shard_map(shards, mesh=mesh, in_specs=in_specs, out_specs=out_specs, check_vma=False)
```

```python
import jax
import jax.numpy as jnp
from jax import lax
from jax.experimental import pallas as pl
from jax.experimental.pallas import tpu as pltpu
from jax.sharding import PartitionSpec as P

CHEB = 6


shift_mass = 1.0
lower_edge = 1.0
upper_edge = 144.0
highest = lax.Precision.HIGHEST
f32 = jnp.float32
VMEM_LIMIT = 20 * 1024 * 1024


def sweep_factors():
    centre = 0.5 * (upper_edge + lower_edge)
    half_range = 0.5 * (upper_edge - lower_edge)
    sigma_ratio = centre / half_range
    rho_now = 1.0 / sigma_ratio
    factors = []
    for sweep_index in range(CHEB):
        rho_next = 1.0 / (2.0 * sigma_ratio - rho_now)
        factors.append((rho_next * rho_now, 2.0 * rho_next / half_range))
        rho_now = rho_next
    return 1.0 / centre, factors


def dot(a, b, dims=((1,), (0,))):
    return lax.dot_general(a, b, (dims, ((), ())), precision=highest, preferred_element_type=f32)


def solve_kernel(
    kappa,
    labels,
    residual,
    first,
    slack,
    row_first,
    row_last,
    col_first,
    col_last,
    root_out,
    zs,
    wide,
    rhs,
    coef,
):
    n, m = labels.shape
    here = labels[...]
    kap = jnp.full(here.shape, kappa[0], f32)
    for region in range(1, kappa.shape[0]):
        kap = jnp.where(here == region, kappa[region], kap)
    root_out[...] = jnp.sqrt(kap)
    kap_t = kap.T
    scale, factors = sweep_factors()
    lanes = residual.shape[2]
    zero_row = jnp.zeros((8, lanes), f32)
    for buffer in (rhs, zs):
        buffer[0] = jnp.zeros(zs.shape[1:], f32)
        buffer[n + 1] = jnp.zeros(zs.shape[1:], f32)
        for i in range(1, n + 1):
            buffer[i, 0:8] = zero_row
            buffer[i, 8 + m :] = zero_row

    for i in range(n):
        spread = jnp.broadcast_to(kap_t[:, i : i + 1], (m, lanes))
        coef[i] = spread
        rhs[i + 1, 8 : 8 + m] = (spread * lax.rsqrt(spread)) * residual[i]

    def neighbours(source, i, before, here_row):
        after = source[i + 2, 8 : 8 + m]
        beside = (before + after) + (source[i + 1, 7 : 7 + m] + source[i + 1, 9 : 9 + m])
        return after, coef[i] * (beside - (4.0 + shift_mass) * here_row)

    unroll = 4
    for sweep, (keep, add) in enumerate(factors):

        def some_rows(block, carry, sweep=sweep, keep=keep, add=add):
            before, here_row = carry
            for step in range(unroll):
                i = block * unroll + step
                if sweep == 0:
                    after, product = neighbours(rhs, i, before, here_row)
                    moved = (keep * scale + add) * here_row + (add * scale) * product
                    zs[i + 1, 8 : 8 + m] = scale * here_row + moved
                else:
                    after, product = neighbours(zs, i, before, here_row)
                    moved = keep * wide[i] + add * (rhs[i + 1, 8 : 8 + m] + product)
                    zs[i + 1, 8 : 8 + m] = here_row + moved
                wide[i] = moved
                before, here_row = here_row, after
            return before, here_row

        source = rhs if sweep == 0 else zs
        lax.fori_loop(0, n // unroll, some_rows, (jnp.zeros((m, lanes), f32), source[1, 8 : 8 + m]))

    before, here_row = jnp.zeros((m, lanes), f32), zs[1, 8 : 8 + m]
    row_first[...] = here_row
    row_last[...] = zs[n, 8 : 8 + m]
    for i in range(n):
        after, product = neighbours(zs, i, before, here_row)
        inv = lax.rsqrt(coef[i])
        slack[i] = (rhs[i + 1, 8 : 8 + m] + product) * inv
        first[i] = here_row * inv
        col_first[i : i + 1] = here_row[0:1]
        col_last[i : i + 1] = here_row[m - 1 : m]
        before, here_row = here_row, after


def solve(residual, labels, region_kappa):
    n, m, lanes = residual.shape
    field = jax.ShapeDtypeStruct((n, m, lanes), f32)
    edge_x = jax.ShapeDtypeStruct((m, lanes), f32)
    edge_y = jax.ShapeDtypeStruct((n, lanes), f32)
    whole = pl.BlockSpec(memory_space=pltpu.VMEM)
    return pl.pallas_call(
        solve_kernel,
        out_shape=(field, field, edge_x, edge_x, edge_y, edge_y, jax.ShapeDtypeStruct((n, m), f32)),
        in_specs=[
            pl.BlockSpec(memory_space=pltpu.SMEM),
            whole,
            whole,
        ],
        out_specs=[whole] * 7,
        scratch_shapes=[
            pltpu.VMEM((n + 2, m + 16, lanes), f32),
            pltpu.VMEM((n, m, lanes), f32),
            pltpu.VMEM((n + 2, m + 16, lanes), f32),
            pltpu.VMEM((n, m, lanes), f32),
        ],
        compiler_params=pltpu.CompilerParams(vmem_limit_bytes=VMEM_LIMIT),
        cost_estimate=pl.CostEstimate(
            flops=80 * n * m * lanes, bytes_accessed=12 * n * m * lanes, transcendentals=0
        ),
        name="solve",
    )(region_kappa, labels, residual)


def chosen_cells(primal, width):
    function = lax.broadcasted_iota(jnp.int32, (primal.shape[0], width), 0)
    cells = jnp.full(function.shape, primal[0], jnp.int32)
    for k in range(1, primal.shape[0]):
        cells = jnp.where(function == k, primal[k], cells)
    return cells


def inner_kernel(primal, basis, slack, out):
    cell = lax.broadcasted_iota(jnp.int32, basis.shape, 1)
    weights = basis[...] + jnp.where(cell == chosen_cells(primal, basis.shape[1]), 1.0, 0.0)
    out[...] = dot(weights, slack[...])


def restrict_kernel(
    primal,
    partial,
    basis,
    basis_first,
    basis_last,
    root,
    row_low,
    row_high,
    col_low,
    col_high,
    restrict,
    permuted,
    out,
):
    n, m = root.shape
    here = root[...]
    turned = here.T
    last = (n - 1) * m

    def share(weights, begin, stride, scale, halo):
        cell = begin + stride * lax.broadcasted_iota(jnp.int32, weights.shape, 1)
        weights = weights + jnp.where(cell == chosen_cells(primal, weights.shape[1]), 1.0, 0.0)
        return dot(weights * scale, halo[...])

    coarse_res = (
        partial[...]
        + (share(basis[:, 0:m], 0, 1, here[0:1], row_low) + share(basis[:, last:], last, 1, here[n - 1 :], row_high))
        + (
            share(basis_first[...], 0, m, turned[0:1], col_low)
            + share(basis_last[...], m - 1, m, turned[m - 1 :], col_high)
        )
    )
    terms = dot(restrict[...], coarse_res, ((0,), (0,)))
    both = jnp.concatenate([coarse_res, terms], axis=0)
    for member in range(out.shape[0]):
        out[member] = both


def row_kernel(everyone, local_two, two, out):
    members, height, lanes = everyone.shape
    count = two.shape[0]
    values = jnp.concatenate([everyone[member, 0:count] for member in range(members)], axis=0)
    two[...] = dot(local_two[...], values)
    terms = everyone[0, count:]
    for member in range(1, members):
        terms = terms + everyone[member, count:]
    for member in range(out.shape[0]):
        out[member] = terms


def split(values):
    high = values.astype(jnp.bfloat16).astype(f32)
    rest = values - high
    mid = rest.astype(jnp.bfloat16).astype(f32)
    return high, mid, rest - mid


def correct_kernel(terms, level_three, restrict, two, basis, first, result, held, sem):
    members, height, lanes = terms.shape
    placed = jnp.concatenate([terms[member] for member in range(members)], axis=0)
    three = dot(level_three[...], placed)
    coarse = two[...] + dot(restrict[...], three)
    c0, c1, c2 = split(coarse)
    right = jnp.concatenate([c0, c1, c2, c0, c1, c0], axis=0).astype(jnp.bfloat16)
    pieces = sem.shape[0]
    cells = held.shape[0] // pieces
    copies = []
    for piece in range(pieces):
        at = pl.ds(piece * cells, cells)
        b0, b1, b2 = split(basis[:, piece * cells : (piece + 1) * cells])
        left = jnp.concatenate([b0, b0, b0, b1, b1, b2], axis=0).T.astype(jnp.bfloat16)
        held[at] = first[at] + jnp.dot(left, right, preferred_element_type=f32)
        copy = pltpu.make_async_copy(held.at[at], result.at[at], sem.at[piece])
        copy.start()
        copies.append(copy)
    for copy in copies:
        copy.wait()


def vmem_call(body, out_shape, inputs, name, scalars=0):
    whole = pl.BlockSpec(memory_space=pltpu.VMEM)
    return pl.pallas_call(
        body,
        out_shape=out_shape,
        in_specs=[pl.BlockSpec(memory_space=pltpu.SMEM)] * scalars + [whole] * (len(inputs) - scalars),
        out_specs=jax.tree.map(lambda _: whole, out_shape),
        compiler_params=pltpu.CompilerParams(vmem_limit_bytes=VMEM_LIMIT),
        name=name,
    )(*inputs)


def shards(
    residual,
    labels,
    region_kappa,
    coarse_basis,
    primal_cells,
    level_two,
    row_restrict,
    level_three,
    row_order,
):
    cells_x, cells_y, rhs_count = residual.shape
    coarse_count = coarse_basis.shape[0]
    cell_count = cells_x * cells_y
    local_two = level_two[0]
    local_restrict = row_restrict[0]
    coarse_third = local_restrict.shape[1]
    members_x, members_y = lax.axis_size("sx"), lax.axis_size("sy")

    first, slack, row_first, row_last, col_first, col_last, root = solve(residual, labels, region_kappa)

    def sent(edge, axis, up):
        count = lax.axis_size(axis)
        pairs = [(i, i + 1) if up else (i + 1, i) for i in range(count - 1)]
        return lax.ppermute(edge, axis, pairs)

    row_low, row_high = sent(row_last, "sx", True), sent(row_first, "sx", False)
    col_low, col_high = sent(col_last, "sy", True), sent(col_first, "sy", False)

    primal = primal_cells.reshape(-1)
    basis_cells = coarse_basis.reshape(coarse_count, cell_count)
    partial = vmem_call(
        inner_kernel,
        jax.ShapeDtypeStruct((coarse_count, rhs_count), f32),
        (primal, basis_cells, slack.reshape(cell_count, rhs_count)),
        "inner",
        scalars=1,
    )
    order_table = (
        row_order[None, :] == jnp.arange(row_order.shape[0], dtype=jnp.int32)[:, None]
    ).astype(f32)
    permuted = jnp.dot(level_three, order_table, precision=highest)

    copies = vmem_call(
        restrict_kernel,
        jax.ShapeDtypeStruct((members_y, coarse_count + coarse_third, rhs_count), f32),
        (
            primal,
            partial,
            basis_cells,
            coarse_basis[:, :, 0],
            coarse_basis[:, :, -1],
            root,
            row_low,
            row_high,
            col_low,
            col_high,
            local_restrict,
            permuted,
        ),
        "restrict",
        scalars=1,
    )
    everyone = lax.all_to_all(copies, "sy", 0, 0, tiled=True)
    two, copies = vmem_call(
        row_kernel,
        (
            jax.ShapeDtypeStruct((coarse_count, rhs_count), f32),
            jax.ShapeDtypeStruct((members_x, coarse_third, rhs_count), f32),
        ),
        (everyone, local_two),
        "row",
    )
    terms = lax.all_to_all(copies, "sx", 0, 0, tiled=True)

    whole = pl.BlockSpec(memory_space=pltpu.VMEM)
    result = pl.pallas_call(
        correct_kernel,
        out_shape=jax.ShapeDtypeStruct((cell_count, rhs_count), f32),
        in_specs=[whole] * 6,
        out_specs=pl.BlockSpec(memory_space=pl.ANY),
        scratch_shapes=[pltpu.VMEM((cell_count, rhs_count), f32), pltpu.SemaphoreType.DMA((6,))],
        compiler_params=pltpu.CompilerParams(vmem_limit_bytes=VMEM_LIMIT),
        name="correct",
    )(terms, permuted, local_restrict, two, basis_cells, first.reshape(cell_count, rhs_count))
    return result.reshape(cells_x, cells_y, rhs_count)


def solution(mesh):
    in_specs = (
        P("sx", "sy", None),
        P("sx", "sy"),
        P(),
        P(None, "sx", "sy"),
        P("sx", "sy", None),
        P("sx", "sy", None),
        P("sx", "sy", None),
        P("sx", None),
        P(),
    )
    out_specs = P("sx", "sy", None)
    return jax.shard_map(shards, mesh=mesh, in_specs=in_specs, out_specs=out_specs, check_vma=False)
```

```python
import jax
import jax.numpy as jnp
from jax import lax
from jax.experimental import pallas as pl
from jax.experimental.pallas import tpu as pltpu
from jax.sharding import PartitionSpec as P

CHEB = 6


shift_mass = 1.0
lower_edge = 1.0
upper_edge = 144.0
highest = lax.Precision.HIGHEST
f32 = jnp.float32
VMEM_LIMIT = 20 * 1024 * 1024


def sweep_factors():
    centre = 0.5 * (upper_edge + lower_edge)
    half_range = 0.5 * (upper_edge - lower_edge)
    sigma_ratio = centre / half_range
    rho_now = 1.0 / sigma_ratio
    factors = []
    for sweep_index in range(CHEB):
        rho_next = 1.0 / (2.0 * sigma_ratio - rho_now)
        factors.append((rho_next * rho_now, 2.0 * rho_next / half_range))
        rho_now = rho_next
    return 1.0 / centre, factors


def dot(a, b, dims=((1,), (0,))):
    return lax.dot_general(a, b, (dims, ((), ())), precision=highest, preferred_element_type=f32)


def solve_kernel(
    kappa_hbm,
    labels,
    residual,
    first,
    slack,
    row_far,
    row_near,
    col_far,
    col_near,
    root_out,
    zs,
    wide,
    rhs,
    coef,
    loaded,
    kinds,
    kappa,
    load_sem,
):
    n, m = labels.shape
    parts = load_sem.shape[0] - 2
    rows = n // parts
    kinds_copy = pltpu.make_async_copy(labels, kinds, load_sem.at[parts])
    kinds_copy.start()
    kappa_copy = pltpu.make_async_copy(kappa_hbm, kappa, load_sem.at[parts + 1])
    kappa_copy.start()
    loads = [
        pltpu.make_async_copy(
            residual.at[pl.ds(p * rows, rows)], loaded.at[pl.ds(p * rows, rows)], load_sem.at[p]
        )
        for p in range(parts)
    ]
    for copy in loads:
        copy.start()
    scale, factors = sweep_factors()
    lanes = residual.shape[2]
    zero_row = jnp.zeros((8, lanes), f32)
    for buffer in (rhs, zs):
        buffer[0] = jnp.zeros(zs.shape[1:], f32)
        buffer[n + 1] = jnp.zeros(zs.shape[1:], f32)
        for i in range(1, n + 1):
            buffer[i, 0:8] = zero_row
            buffer[i, 8 + m :] = zero_row

    kinds_copy.wait()
    kappa_copy.wait()
    here = kinds[...]
    kap = jnp.full(here.shape, kappa[0], f32)
    for region in range(1, kappa.shape[0]):
        kap = jnp.where(here == region, kappa[region], kap)
    root_out[...] = jnp.sqrt(kap)
    kap_t = kap.T
    for i in range(n):
        if i % rows == 0:
            loads[i // rows].wait()
        spread = jnp.broadcast_to(kap_t[:, i : i + 1], (m, lanes))
        coef[i] = spread
        rhs[i + 1, 8 : 8 + m] = (spread * lax.rsqrt(spread)) * loaded[i]

    def neighbours(source, i, before, here_row):
        after = source[i + 2, 8 : 8 + m]
        beside = (before + after) + (source[i + 1, 7 : 7 + m] + source[i + 1, 9 : 9 + m])
        return after, coef[i] * (beside - (4.0 + shift_mass) * here_row)

    unroll = 4
    for sweep, (keep, add) in enumerate(factors):

        def some_rows(block, carry, sweep=sweep, keep=keep, add=add):
            before, here_row = carry
            for step in range(unroll):
                i = block * unroll + step
                if sweep == 0:
                    after, product = neighbours(rhs, i, before, here_row)
                    moved = (keep * scale + add) * here_row + (add * scale) * product
                    zs[i + 1, 8 : 8 + m] = scale * here_row + moved
                else:
                    after, product = neighbours(zs, i, before, here_row)
                    moved = keep * wide[i] + add * (rhs[i + 1, 8 : 8 + m] + product)
                    zs[i + 1, 8 : 8 + m] = here_row + moved
                wide[i] = moved
                before, here_row = here_row, after
            return before, here_row

        source = rhs if sweep == 0 else zs
        lax.fori_loop(0, n // unroll, some_rows, (jnp.zeros((m, lanes), f32), source[1, 8 : 8 + m]))

    before, here_row = jnp.zeros((m, lanes), f32), zs[1, 8 : 8 + m]
    even_x = lax.rem(lax.axis_index("sx"), 2) == 0
    even_y = lax.rem(lax.axis_index("sy"), 2) == 0
    row_last = zs[n, 8 : 8 + m]
    row_far[...] = jnp.where(even_x, here_row, row_last)
    row_near[...] = jnp.where(even_x, row_last, here_row)
    for i in range(n):
        after, product = neighbours(zs, i, before, here_row)
        inv = lax.rsqrt(coef[i])
        slack[i] = (rhs[i + 1, 8 : 8 + m] + product) * inv
        first[i] = here_row * inv
        col_far[i : i + 1] = here_row[0:1]
        col_near[i : i + 1] = here_row[m - 1 : m]
        before, here_row = here_row, after
    col_first, col_last = col_far[...], col_near[...]
    col_far[...] = jnp.where(even_y, col_first, col_last)
    col_near[...] = jnp.where(even_y, col_last, col_first)


def solve(residual, labels, region_kappa):
    n, m, lanes = residual.shape
    field = jax.ShapeDtypeStruct((n, m, lanes), f32)
    edge_x = jax.ShapeDtypeStruct((m, lanes), f32)
    edge_y = jax.ShapeDtypeStruct((n, lanes), f32)
    whole = pl.BlockSpec(memory_space=pltpu.VMEM)
    return pl.pallas_call(
        solve_kernel,
        out_shape=(field, field, edge_x, edge_x, edge_y, edge_y, jax.ShapeDtypeStruct((n, m), f32)),
        in_specs=[
            pl.BlockSpec(memory_space=pltpu.HBM),
            pl.BlockSpec(memory_space=pltpu.HBM),
            pl.BlockSpec(memory_space=pltpu.HBM),
        ],
        out_specs=[whole] * 7,
        scratch_shapes=[
            pltpu.VMEM((n + 2, m + 16, lanes), f32),
            pltpu.VMEM((n, m, lanes), f32),
            pltpu.VMEM((n + 2, m + 16, lanes), f32),
            pltpu.VMEM((n, m, lanes), f32),
            pltpu.VMEM((n, m, lanes), f32),
            pltpu.VMEM((n, m), jnp.int32),
            pltpu.SMEM(region_kappa.shape, f32),
            pltpu.SemaphoreType.DMA((6,)),
        ],
        compiler_params=pltpu.CompilerParams(vmem_limit_bytes=VMEM_LIMIT),
        cost_estimate=pl.CostEstimate(
            flops=80 * n * m * lanes, bytes_accessed=12 * n * m * lanes, transcendentals=0
        ),
        name="solve",
    )(
        pltpu.with_memory_space_constraint(region_kappa, pltpu.HBM),
        pltpu.with_memory_space_constraint(labels, pltpu.HBM),
        pltpu.with_memory_space_constraint(residual, pltpu.HBM),
    )


def chosen_cells(primal, width):
    function = lax.broadcasted_iota(jnp.int32, (primal.shape[0], width), 0)
    cells = jnp.full(function.shape, primal[0], jnp.int32)
    for k in range(1, primal.shape[0]):
        cells = jnp.where(function == k, primal[k], cells)
    return cells


def inner_kernel(primal, basis, slack, out):
    cell = lax.broadcasted_iota(jnp.int32, basis.shape, 1)
    weights = basis[...] + jnp.where(cell == chosen_cells(primal, basis.shape[1]), 1.0, 0.0)
    out[...] = dot(weights, slack[...])


def restrict_kernel(
    primal,
    partial,
    basis,
    basis_first,
    basis_last,
    root,
    row_far,
    row_near,
    col_far,
    col_near,
    restrict,
    permuted,
    out,
):
    n, m = root.shape
    even_x = lax.rem(lax.axis_index("sx"), 2) == 0
    even_y = lax.rem(lax.axis_index("sy"), 2) == 0
    row_low = jnp.where(even_x, row_far[...], row_near[...])
    row_high = jnp.where(even_x, row_near[...], row_far[...])
    col_low = jnp.where(even_y, col_far[...], col_near[...])
    col_high = jnp.where(even_y, col_near[...], col_far[...])
    here = root[...]
    turned = here.T
    last = (n - 1) * m

    def share(weights, begin, stride, scale, halo):
        cell = begin + stride * lax.broadcasted_iota(jnp.int32, weights.shape, 1)
        weights = weights + jnp.where(cell == chosen_cells(primal, weights.shape[1]), 1.0, 0.0)
        return dot(weights * scale, halo)

    coarse_res = (
        partial[...]
        + (share(basis[:, 0:m], 0, 1, here[0:1], row_low) + share(basis[:, last:], last, 1, here[n - 1 :], row_high))
        + (
            share(basis_first[...], 0, m, turned[0:1], col_low)
            + share(basis_last[...], m - 1, m, turned[m - 1 :], col_high)
        )
    )
    terms = dot(restrict[...], coarse_res, ((0,), (0,)))
    both = jnp.concatenate([coarse_res, terms], axis=0)
    for member in range(out.shape[0]):
        out[member] = both


def row_kernel(everyone, local_two, two, out):
    members, height, lanes = everyone.shape
    count = two.shape[0]
    values = jnp.concatenate([everyone[member, 0:count] for member in range(members)], axis=0)
    two[...] = dot(local_two[...], values)
    terms = everyone[0, count:]
    for member in range(1, members):
        terms = terms + everyone[member, count:]
    for member in range(out.shape[0]):
        out[member] = terms


def split(values):
    high = values.astype(jnp.bfloat16).astype(f32)
    rest = values - high
    mid = rest.astype(jnp.bfloat16).astype(f32)
    return high, mid, rest - mid


def correct_kernel(terms, level_three, restrict, two, basis, first, result, held, sem):
    members, height, lanes = terms.shape
    placed = jnp.concatenate([terms[member] for member in range(members)], axis=0)
    three = dot(level_three[...], placed)
    coarse = two[...] + dot(restrict[...], three)
    c0, c1, c2 = split(coarse)
    right = jnp.concatenate([c0, c1, c2, c0, c1, c0], axis=0).astype(jnp.bfloat16)
    pieces = sem.shape[0]
    cells = held.shape[0] // pieces
    copies = []
    for piece in range(pieces):
        at = pl.ds(piece * cells, cells)
        b0, b1, b2 = split(basis[:, piece * cells : (piece + 1) * cells])
        left = jnp.concatenate([b0, b0, b0, b1, b1, b2], axis=0).T.astype(jnp.bfloat16)
        held[at] = first[at] + jnp.dot(left, right, preferred_element_type=f32)
        copy = pltpu.make_async_copy(held.at[at], result.at[at], sem.at[piece])
        copy.start()
        copies.append(copy)
    for copy in copies:
        copy.wait()


def vmem_call(body, out_shape, inputs, name, scalars=0):
    whole = pl.BlockSpec(memory_space=pltpu.VMEM)
    return pl.pallas_call(
        body,
        out_shape=out_shape,
        in_specs=[pl.BlockSpec(memory_space=pltpu.SMEM)] * scalars + [whole] * (len(inputs) - scalars),
        out_specs=jax.tree.map(lambda _: whole, out_shape),
        compiler_params=pltpu.CompilerParams(vmem_limit_bytes=VMEM_LIMIT),
        name=name,
    )(*inputs)


def shards(
    residual,
    labels,
    region_kappa,
    coarse_basis,
    primal_cells,
    level_two,
    row_restrict,
    level_three,
    row_order,
):
    cells_x, cells_y, rhs_count = residual.shape
    coarse_count = coarse_basis.shape[0]
    cell_count = cells_x * cells_y
    local_two = level_two[0]
    local_restrict = row_restrict[0]
    coarse_third = local_restrict.shape[1]
    members_x, members_y = lax.axis_size("sx"), lax.axis_size("sy")

    first, slack, row_far, row_near, col_far, col_near, root = solve(residual, labels, region_kappa)

    def swapped(edge, axis, begin):
        count = lax.axis_size(axis)
        pairs = [(i, i + 1) for i in range(begin, count - 1, 2)]
        return lax.ppermute(edge, axis, pairs + [(target, source) for source, target in pairs])

    row_far = swapped(row_far, "sx", 1)
    col_far = swapped(col_far, "sy", 1)
    row_near = swapped(row_near, "sx", 0)
    col_near = swapped(col_near, "sy", 0)

    primal = primal_cells.reshape(-1)
    basis_cells = coarse_basis.reshape(coarse_count, cell_count)
    partial = vmem_call(
        inner_kernel,
        jax.ShapeDtypeStruct((coarse_count, rhs_count), f32),
        (primal, basis_cells, slack.reshape(cell_count, rhs_count)),
        "inner",
        scalars=1,
    )
    order_table = (
        row_order[None, :] == jnp.arange(row_order.shape[0], dtype=jnp.int32)[:, None]
    ).astype(f32)
    permuted = jnp.dot(level_three, order_table, precision=highest)

    copies = vmem_call(
        restrict_kernel,
        jax.ShapeDtypeStruct((members_y, coarse_count + coarse_third, rhs_count), f32),
        (
            primal,
            partial,
            basis_cells,
            coarse_basis[:, :, 0],
            coarse_basis[:, :, -1],
            root,
            row_far,
            row_near,
            col_far,
            col_near,
            local_restrict,
            permuted,
        ),
        "restrict",
        scalars=1,
    )
    everyone = lax.all_to_all(copies, "sy", 0, 0, tiled=True)
    two, copies = vmem_call(
        row_kernel,
        (
            jax.ShapeDtypeStruct((coarse_count, rhs_count), f32),
            jax.ShapeDtypeStruct((members_x, coarse_third, rhs_count), f32),
        ),
        (everyone, local_two),
        "row",
    )
    terms = lax.all_to_all(copies, "sx", 0, 0, tiled=True)

    whole = pl.BlockSpec(memory_space=pltpu.VMEM)
    result = pl.pallas_call(
        correct_kernel,
        out_shape=jax.ShapeDtypeStruct((cell_count, rhs_count), f32),
        in_specs=[whole] * 6,
        out_specs=pl.BlockSpec(memory_space=pl.ANY),
        scratch_shapes=[pltpu.VMEM((cell_count, rhs_count), f32), pltpu.SemaphoreType.DMA((6,))],
        compiler_params=pltpu.CompilerParams(vmem_limit_bytes=VMEM_LIMIT),
        name="correct",
    )(terms, permuted, local_restrict, two, basis_cells, first.reshape(cell_count, rhs_count))
    return result.reshape(cells_x, cells_y, rhs_count)


def solution(mesh):
    in_specs = (
        P("sx", "sy", None),
        P("sx", "sy"),
        P(),
        P(None, "sx", "sy"),
        P("sx", "sy", None),
        P("sx", "sy", None),
        P("sx", "sy", None),
        P("sx", None),
        P(),
    )
    out_specs = P("sx", "sy", None)
    return jax.shard_map(shards, mesh=mesh, in_specs=in_specs, out_specs=out_specs, check_vma=False)
```

```python
import jax
import jax.numpy as jnp
from jax import lax
from jax.experimental import pallas as pl
from jax.experimental.pallas import tpu as pltpu
from jax.sharding import PartitionSpec as P

CHEB = 6


shift_mass = 1.0
lower_edge = 1.0
upper_edge = 144.0
highest = lax.Precision.HIGHEST
f32 = jnp.float32
VMEM_LIMIT = 20 * 1024 * 1024


def sweep_factors():
    centre = 0.5 * (upper_edge + lower_edge)
    half_range = 0.5 * (upper_edge - lower_edge)
    sigma_ratio = centre / half_range
    rho_now = 1.0 / sigma_ratio
    factors = []
    for sweep_index in range(CHEB):
        rho_next = 1.0 / (2.0 * sigma_ratio - rho_now)
        factors.append((rho_next * rho_now, 2.0 * rho_next / half_range))
        rho_now = rho_next
    return 1.0 / centre, factors


def dot(a, b, dims=((1,), (0,))):
    return lax.dot_general(a, b, (dims, ((), ())), precision=highest, preferred_element_type=f32)


def solve_kernel(
    kappa_hbm,
    labels,
    residual,
    first,
    slack,
    row_far,
    col_far,
    row_near,
    col_near,
    root_out,
    zs,
    wide,
    rhs,
    coef,
    loaded,
    kinds,
    kappa,
    load_sem,
):
    n, m = labels.shape
    parts = load_sem.shape[0] - 2
    rows = n // parts
    kinds_copy = pltpu.make_async_copy(labels, kinds, load_sem.at[parts])
    kinds_copy.start()
    kappa_copy = pltpu.make_async_copy(kappa_hbm, kappa, load_sem.at[parts + 1])
    kappa_copy.start()
    loads = [
        pltpu.make_async_copy(
            residual.at[pl.ds(p * rows, rows)], loaded.at[pl.ds(p * rows, rows)], load_sem.at[p]
        )
        for p in range(parts)
    ]
    for copy in loads:
        copy.start()
    scale, factors = sweep_factors()
    lanes = residual.shape[2]
    zero_row = jnp.zeros((8, lanes), f32)
    for buffer in (rhs, zs):
        buffer[0] = jnp.zeros(zs.shape[1:], f32)
        buffer[n + 1] = jnp.zeros(zs.shape[1:], f32)
        for i in range(1, n + 1):
            buffer[i, 0:8] = zero_row
            buffer[i, 8 + m :] = zero_row

    kinds_copy.wait()
    kappa_copy.wait()
    here = kinds[...]
    kap = jnp.full(here.shape, kappa[0], f32)
    for region in range(1, kappa.shape[0]):
        kap = jnp.where(here == region, kappa[region], kap)
    root_out[...] = jnp.sqrt(kap)
    kap_t = kap.T
    for i in range(n):
        if i % rows == 0:
            loads[i // rows].wait()
        spread = jnp.broadcast_to(kap_t[:, i : i + 1], (m, lanes))
        coef[i] = spread
        rhs[i + 1, 8 : 8 + m] = (spread * lax.rsqrt(spread)) * loaded[i]

    def neighbours(source, i, before, here_row):
        after = source[i + 2, 8 : 8 + m]
        beside = (before + after) + (source[i + 1, 7 : 7 + m] + source[i + 1, 9 : 9 + m])
        return after, coef[i] * (beside - (4.0 + shift_mass) * here_row)

    unroll = 4
    for sweep, (keep, add) in enumerate(factors):

        def some_rows(block, carry, sweep=sweep, keep=keep, add=add):
            before, here_row = carry
            for step in range(unroll):
                i = block * unroll + step
                if sweep == 0:
                    after, product = neighbours(rhs, i, before, here_row)
                    moved = (keep * scale + add) * here_row + (add * scale) * product
                    zs[i + 1, 8 : 8 + m] = scale * here_row + moved
                else:
                    after, product = neighbours(zs, i, before, here_row)
                    moved = keep * wide[i] + add * (rhs[i + 1, 8 : 8 + m] + product)
                    zs[i + 1, 8 : 8 + m] = here_row + moved
                wide[i] = moved
                before, here_row = here_row, after
            return before, here_row

        source = rhs if sweep == 0 else zs
        lax.fori_loop(0, n // unroll, some_rows, (jnp.zeros((m, lanes), f32), source[1, 8 : 8 + m]))

    before, here_row = jnp.zeros((m, lanes), f32), zs[1, 8 : 8 + m]
    even_x = lax.rem(lax.axis_index("sx"), 2) == 0
    even_y = lax.rem(lax.axis_index("sy"), 2) == 0
    row_last = zs[n, 8 : 8 + m]
    row_far[...] = jnp.where(even_x, here_row, row_last)
    row_near[...] = jnp.where(even_x, row_last, here_row)
    for i in range(n):
        after, product = neighbours(zs, i, before, here_row)
        inv = lax.rsqrt(coef[i])
        slack[i] = (rhs[i + 1, 8 : 8 + m] + product) * inv
        first[i] = here_row * inv
        col_far[i : i + 1] = here_row[0:1]
        col_near[i : i + 1] = here_row[m - 1 : m]
        before, here_row = here_row, after
    col_first, col_last = col_far[...], col_near[...]
    col_far[...] = jnp.where(even_y, col_first, col_last)
    col_near[...] = jnp.where(even_y, col_last, col_first)


def solve(residual, labels, region_kappa):
    n, m, lanes = residual.shape
    field = jax.ShapeDtypeStruct((n, m, lanes), f32)
    edge_x = jax.ShapeDtypeStruct((m, lanes), f32)
    edge_y = jax.ShapeDtypeStruct((n, lanes), f32)
    whole = pl.BlockSpec(memory_space=pltpu.VMEM)
    return pl.pallas_call(
        solve_kernel,
        out_shape=(field, field, edge_x, edge_y, edge_x, edge_y, jax.ShapeDtypeStruct((n, m), f32)),
        in_specs=[
            pl.BlockSpec(memory_space=pltpu.HBM),
            pl.BlockSpec(memory_space=pltpu.HBM),
            pl.BlockSpec(memory_space=pltpu.HBM),
        ],
        out_specs=[whole] * 7,
        scratch_shapes=[
            pltpu.VMEM((n + 2, m + 16, lanes), f32),
            pltpu.VMEM((n, m, lanes), f32),
            pltpu.VMEM((n + 2, m + 16, lanes), f32),
            pltpu.VMEM((n, m, lanes), f32),
            pltpu.VMEM((n, m, lanes), f32),
            pltpu.VMEM((n, m), jnp.int32),
            pltpu.SMEM(region_kappa.shape, f32),
            pltpu.SemaphoreType.DMA((6,)),
        ],
        compiler_params=pltpu.CompilerParams(vmem_limit_bytes=VMEM_LIMIT),
        cost_estimate=pl.CostEstimate(
            flops=80 * n * m * lanes, bytes_accessed=12 * n * m * lanes, transcendentals=0
        ),
        name="solve",
    )(
        pltpu.with_memory_space_constraint(region_kappa, pltpu.HBM),
        pltpu.with_memory_space_constraint(labels, pltpu.HBM),
        pltpu.with_memory_space_constraint(residual, pltpu.HBM),
    )


def chosen_cells(primal, width):
    function = lax.broadcasted_iota(jnp.int32, (primal.shape[0], width), 0)
    cells = jnp.full(function.shape, primal[0], jnp.int32)
    for k in range(1, primal.shape[0]):
        cells = jnp.where(function == k, primal[k], cells)
    return cells


def inner_kernel(primal, basis, slack, out):
    cell = lax.broadcasted_iota(jnp.int32, basis.shape, 1)
    weights = basis[...] + jnp.where(cell == chosen_cells(primal, basis.shape[1]), 1.0, 0.0)
    out[...] = dot(weights, slack[...])


def restrict_kernel(
    primal,
    partial,
    basis,
    basis_first,
    basis_last,
    root,
    row_far,
    col_far,
    row_near,
    col_near,
    restrict,
    permuted,
    out,
):
    n, m = root.shape
    even_x = lax.rem(lax.axis_index("sx"), 2) == 0
    even_y = lax.rem(lax.axis_index("sy"), 2) == 0
    row_low = jnp.where(even_x, row_far[...], row_near[...])
    row_high = jnp.where(even_x, row_near[...], row_far[...])
    col_low = jnp.where(even_y, col_far[...], col_near[...])
    col_high = jnp.where(even_y, col_near[...], col_far[...])
    here = root[...]
    turned = here.T
    last = (n - 1) * m

    def share(weights, begin, stride, scale):
        cell = begin + stride * lax.broadcasted_iota(jnp.int32, weights.shape, 1)
        chosen = jnp.where(cell == chosen_cells(primal, weights.shape[1]), 1.0, 0.0)
        return (weights + chosen) * scale

    weights = jnp.concatenate(
        [
            share(basis[:, 0:m], 0, 1, here[0:1]),
            share(basis[:, last:], last, 1, here[n - 1 :]),
            share(basis_first[...], 0, m, turned[0:1]),
            share(basis_last[...], m - 1, m, turned[m - 1 :]),
        ],
        axis=1,
    )
    halo = jnp.concatenate([row_low, row_high, col_low, col_high], axis=0)
    both = jnp.concatenate([partial[...] + dot(weights, halo), restrict[...]], axis=0)
    height = both.shape[0]
    for member in range(out.shape[0] // height):
        out[member * height : (member + 1) * height] = both


def row_kernel(everyone, local_two, two, out):
    count = two.shape[0]
    height = count + 1
    third = out.shape[1]
    members = everyone.shape[0] // height
    values = jnp.concatenate([everyone[m * height : m * height + count] for m in range(members)], axis=0)
    two[...] = dot(local_two[...], values)
    shape = (count, everyone.shape[1])
    own = lax.broadcasted_iota(jnp.int32, shape, 1) // third == lax.broadcasted_iota(jnp.int32, shape, 0)
    spread = jnp.concatenate(
        [
            jnp.where(own, jnp.broadcast_to(everyone[m * height + count : (m + 1) * height], shape), 0.0)
            for m in range(members)
        ],
        axis=0,
    )
    products = dot(spread, values, ((0,), (0,)))
    terms = products[0:third]
    for k in range(1, count):
        terms = terms + products[k * third : (k + 1) * third]
    for member in range(out.shape[0]):
        out[member] = terms


def split(values):
    high = values.astype(jnp.bfloat16).astype(f32)
    rest = values - high
    mid = rest.astype(jnp.bfloat16).astype(f32)
    return high, mid, rest - mid


def correct_kernel(terms, level_three, restrict, two, basis, first, result, held, sem):
    members, height, lanes = terms.shape
    placed = jnp.concatenate([terms[member] for member in range(members)], axis=0)
    three = dot(level_three[...], placed)
    coarse = two[...] + dot(restrict[...], three)
    c0, c1, c2 = split(coarse)
    right = jnp.concatenate([c0, c1, c2, c0, c1, c0], axis=0).astype(jnp.bfloat16)
    pieces = sem.shape[0]
    cells = held.shape[0] // pieces
    copies = []
    for piece in range(pieces):
        at = pl.ds(piece * cells, cells)
        b0, b1, b2 = split(basis[:, piece * cells : (piece + 1) * cells])
        left = jnp.concatenate([b0, b0, b0, b1, b1, b2], axis=0).T.astype(jnp.bfloat16)
        held[at] = first[at] + jnp.dot(left, right, preferred_element_type=f32)
        copy = pltpu.make_async_copy(held.at[at], result.at[at], sem.at[piece])
        copy.start()
        copies.append(copy)
    for copy in copies:
        copy.wait()


def vmem_call(body, out_shape, inputs, name, scalars=0):
    whole = pl.BlockSpec(memory_space=pltpu.VMEM)
    return pl.pallas_call(
        body,
        out_shape=out_shape,
        in_specs=[pl.BlockSpec(memory_space=pltpu.SMEM)] * scalars + [whole] * (len(inputs) - scalars),
        out_specs=jax.tree.map(lambda _: whole, out_shape),
        compiler_params=pltpu.CompilerParams(vmem_limit_bytes=VMEM_LIMIT),
        name=name,
    )(*inputs)


def shards(
    residual,
    labels,
    region_kappa,
    coarse_basis,
    primal_cells,
    level_two,
    row_restrict,
    level_three,
    row_order,
):
    cells_x, cells_y, rhs_count = residual.shape
    coarse_count = coarse_basis.shape[0]
    cell_count = cells_x * cells_y
    local_two = level_two[0]
    local_restrict = row_restrict[0]
    coarse_third = local_restrict.shape[1]
    members_x, members_y = lax.axis_size("sx"), lax.axis_size("sy")

    first, slack, row_far, col_far, row_near, col_near, root = solve(residual, labels, region_kappa)

    def swapped(edge, axis, begin):
        count = lax.axis_size(axis)
        pairs = [(i, i + 1) for i in range(begin, count - 1, 2)]
        return lax.ppermute(edge, axis, pairs + [(target, source) for source, target in pairs])

    row_far = swapped(row_far, "sx", 1)
    col_far = swapped(col_far, "sy", 1)
    row_near = swapped(row_near, "sx", 0)
    col_near = swapped(col_near, "sy", 0)

    primal = primal_cells.reshape(-1)
    basis_cells = coarse_basis.reshape(coarse_count, cell_count)
    partial = vmem_call(
        inner_kernel,
        jax.ShapeDtypeStruct((coarse_count, rhs_count), f32),
        (primal, basis_cells, slack.reshape(cell_count, rhs_count)),
        "inner",
        scalars=1,
    )
    order_table = (
        row_order[None, :] == jnp.arange(row_order.shape[0], dtype=jnp.int32)[:, None]
    ).astype(f32)
    permuted = jnp.dot(level_three, order_table, precision=highest)

    copies = vmem_call(
        restrict_kernel,
        jax.ShapeDtypeStruct((members_y * (coarse_count + 1), rhs_count), f32),
        (
            primal,
            partial,
            basis_cells,
            coarse_basis[:, :, 0],
            coarse_basis[:, :, -1],
            root,
            row_far,
            col_far,
            row_near,
            col_near,
            local_restrict.reshape(1, coarse_count * coarse_third),
            permuted,
        ),
        "restrict",
        scalars=1,
    )
    everyone = lax.all_to_all(copies[:, None], "sy", 0, 0, tiled=True)[:, 0]
    two, copies = vmem_call(
        row_kernel,
        (
            jax.ShapeDtypeStruct((coarse_count, rhs_count), f32),
            jax.ShapeDtypeStruct((members_x, coarse_third, rhs_count), f32),
        ),
        (everyone, local_two),
        "row",
    )
    terms = lax.all_to_all(copies, "sx", 0, 0, tiled=True)

    whole = pl.BlockSpec(memory_space=pltpu.VMEM)
    result = pl.pallas_call(
        correct_kernel,
        out_shape=jax.ShapeDtypeStruct((cell_count, rhs_count), f32),
        in_specs=[whole] * 6,
        out_specs=pl.BlockSpec(memory_space=pl.ANY),
        scratch_shapes=[pltpu.VMEM((cell_count, rhs_count), f32), pltpu.SemaphoreType.DMA((6,))],
        compiler_params=pltpu.CompilerParams(vmem_limit_bytes=VMEM_LIMIT),
        name="correct",
    )(terms, permuted, local_restrict, two, basis_cells, first.reshape(cell_count, rhs_count))
    return result.reshape(cells_x, cells_y, rhs_count)


def solution(mesh):
    in_specs = (
        P("sx", "sy", None),
        P("sx", "sy"),
        P(),
        P(None, "sx", "sy"),
        P("sx", "sy", None),
        P("sx", "sy", None),
        P("sx", "sy", None),
        P("sx", None),
        P(),
    )
    out_specs = P("sx", "sy", None)
    return jax.shard_map(shards, mesh=mesh, in_specs=in_specs, out_specs=out_specs, check_vma=False)
```

```python
import jax
import jax.numpy as jnp
from jax import lax
from jax.experimental import pallas as pl
from jax.experimental.pallas import tpu as pltpu
from jax.sharding import PartitionSpec as P

CHEB = 6


shift_mass = 1.0
lower_edge = 1.0
upper_edge = 144.0
highest = lax.Precision.HIGHEST
f32 = jnp.float32
VMEM_LIMIT = 20 * 1024 * 1024


def sweep_factors():
    centre = 0.5 * (upper_edge + lower_edge)
    half_range = 0.5 * (upper_edge - lower_edge)
    sigma_ratio = centre / half_range
    rho_now = 1.0 / sigma_ratio
    factors = []
    for sweep_index in range(CHEB):
        rho_next = 1.0 / (2.0 * sigma_ratio - rho_now)
        factors.append((rho_next * rho_now, 2.0 * rho_next / half_range))
        rho_now = rho_next
    return 1.0 / centre, factors


def dot(a, b, dims=((1,), (0,))):
    return lax.dot_general(a, b, (dims, ((), ())), precision=highest, preferred_element_type=f32)


def neighbours(source, coef_row, i, before, here_row):
    m = coef_row.shape[0]
    after = source[i + 2, 8 : 8 + m]
    beside = (before + after) + (source[i + 1, 7 : 7 + m] + source[i + 1, 9 : 9 + m])
    return after, coef_row * (beside - (4.0 + shift_mass) * here_row)


def solve_kernel(
    kappa_hbm,
    labels,
    residual,
    zs,
    rhs_out,
    row_far,
    col_far,
    row_near,
    col_near,
    kap_out,
    wide,
    rhs,
    coef,
    loaded,
    kinds,
    kappa,
    load_sem,
):
    n, m = labels.shape
    parts = load_sem.shape[0] - 2
    rows = n // parts
    kinds_copy = pltpu.make_async_copy(labels, kinds, load_sem.at[parts])
    kinds_copy.start()
    kappa_copy = pltpu.make_async_copy(kappa_hbm, kappa, load_sem.at[parts + 1])
    kappa_copy.start()
    loads = [
        pltpu.make_async_copy(
            residual.at[pl.ds(p * rows, rows)], loaded.at[pl.ds(p * rows, rows)], load_sem.at[p]
        )
        for p in range(parts)
    ]
    for copy in loads:
        copy.start()
    scale, factors = sweep_factors()
    lanes = residual.shape[2]
    zero_row = jnp.zeros((8, lanes), f32)
    for buffer in (rhs, zs):
        buffer[0] = jnp.zeros(zs.shape[1:], f32)
        buffer[n + 1] = jnp.zeros(zs.shape[1:], f32)
        for i in range(1, n + 1):
            buffer[i, 0:8] = zero_row
            buffer[i, 8 + m :] = zero_row

    kinds_copy.wait()
    kappa_copy.wait()
    here = kinds[...]
    kap = jnp.full(here.shape, kappa[0], f32)
    for region in range(1, kappa.shape[0]):
        kap = jnp.where(here == region, kappa[region], kap)
    kap_out[...] = kap
    kap_t = kap.T
    for i in range(n):
        if i % rows == 0:
            loads[i // rows].wait()
        spread = jnp.broadcast_to(kap_t[:, i : i + 1], (m, lanes))
        coef[i] = spread
        scaled = (spread * lax.rsqrt(spread)) * loaded[i]
        rhs[i + 1, 8 : 8 + m] = scaled
        rhs_out[i] = scaled

    unroll = 4
    for sweep, (keep, add) in enumerate(factors):

        def some_rows(block, carry, sweep=sweep, keep=keep, add=add):
            before, here_row = carry
            for step in range(unroll):
                i = block * unroll + step
                if sweep == 0:
                    after, product = neighbours(rhs, coef[i], i, before, here_row)
                    moved = (keep * scale + add) * here_row + (add * scale) * product
                    zs[i + 1, 8 : 8 + m] = scale * here_row + moved
                else:
                    after, product = neighbours(zs, coef[i], i, before, here_row)
                    moved = keep * wide[i] + add * (rhs_out[i] + product)
                    zs[i + 1, 8 : 8 + m] = here_row + moved
                wide[i] = moved
                before, here_row = here_row, after
            return before, here_row

        source = rhs if sweep == 0 else zs
        lax.fori_loop(0, n // unroll, some_rows, (jnp.zeros((m, lanes), f32), source[1, 8 : 8 + m]))

    even_x = lax.rem(lax.axis_index("sx"), 2) == 0
    even_y = lax.rem(lax.axis_index("sy"), 2) == 0
    row_first, row_last = zs[1, 8 : 8 + m], zs[n, 8 : 8 + m]
    row_far[...] = jnp.where(even_x, row_first, row_last)
    row_near[...] = jnp.where(even_x, row_last, row_first)
    for i in range(n):
        col_far[i : i + 1] = zs[i + 1, 8:9]
        col_near[i : i + 1] = zs[i + 1, 7 + m : 8 + m]
    col_first, col_last = col_far[...], col_near[...]
    col_far[...] = jnp.where(even_y, col_first, col_last)
    col_near[...] = jnp.where(even_y, col_last, col_first)


def solve(residual, labels, region_kappa):
    n, m, lanes = residual.shape
    field = jax.ShapeDtypeStruct((n, m, lanes), f32)
    framed = jax.ShapeDtypeStruct((n + 2, m + 16, lanes), f32)
    edge_x = jax.ShapeDtypeStruct((m, lanes), f32)
    edge_y = jax.ShapeDtypeStruct((n, lanes), f32)
    whole = pl.BlockSpec(memory_space=pltpu.VMEM)
    return pl.pallas_call(
        solve_kernel,
        out_shape=(framed, field, edge_x, edge_y, edge_x, edge_y, jax.ShapeDtypeStruct((n, m), f32)),
        in_specs=[
            pl.BlockSpec(memory_space=pltpu.HBM),
            pl.BlockSpec(memory_space=pltpu.HBM),
            pl.BlockSpec(memory_space=pltpu.HBM),
        ],
        out_specs=[whole] * 7,
        scratch_shapes=[
            pltpu.VMEM((n, m, lanes), f32),
            pltpu.VMEM((n + 2, m + 16, lanes), f32),
            pltpu.VMEM((n, m, lanes), f32),
            pltpu.VMEM((n, m, lanes), f32),
            pltpu.VMEM((n, m), jnp.int32),
            pltpu.SMEM(region_kappa.shape, f32),
            pltpu.SemaphoreType.DMA((6,)),
        ],
        compiler_params=pltpu.CompilerParams(vmem_limit_bytes=VMEM_LIMIT),
        cost_estimate=pl.CostEstimate(
            flops=80 * n * m * lanes, bytes_accessed=12 * n * m * lanes, transcendentals=0
        ),
        name="solve",
    )(
        pltpu.with_memory_space_constraint(region_kappa, pltpu.HBM),
        pltpu.with_memory_space_constraint(labels, pltpu.HBM),
        pltpu.with_memory_space_constraint(residual, pltpu.HBM),
    )


def chosen_cells(primal, width):
    function = lax.broadcasted_iota(jnp.int32, (primal.shape[0], width), 0)
    cells = jnp.full(function.shape, primal[0], jnp.int32)
    for k in range(1, primal.shape[0]):
        cells = jnp.where(function == k, primal[k], cells)
    return cells


def inner_kernel(
    primal, zs, rhs, basis, fields, kap, out, edge_weights, first, left, slack
):
    n, m, lanes = rhs.shape
    kap_t = kap[...].T
    before, here_row = jnp.zeros((m, lanes), f32), zs[1, 8 : 8 + m]
    for i in range(n):
        spread = jnp.broadcast_to(kap_t[:, i : i + 1], (m, lanes))
        after, product = neighbours(zs, spread, i, before, here_row)
        inv = lax.rsqrt(spread)
        slack[i * m : (i + 1) * m] = (rhs[i] + product) * inv
        first[i * m : (i + 1) * m] = here_row * inv
        before, here_row = here_row, after
    cell = lax.broadcasted_iota(jnp.int32, basis.shape, 1)
    weights = basis[...] + jnp.where(cell == chosen_cells(primal, basis.shape[1]), 1.0, 0.0)
    out[...] = dot(weights, slack[...])

    here = jnp.sqrt(kap[...])
    turned = here.T
    last = (n - 1) * m

    def share(weights, begin, stride, scale):
        cell = begin + stride * lax.broadcasted_iota(jnp.int32, weights.shape, 1)
        chosen = jnp.where(cell == chosen_cells(primal, weights.shape[1]), 1.0, 0.0)
        return (weights + chosen) * scale

    sides = [fields[k].T for k in range(fields.shape[0])]
    basis_first = jnp.concatenate([side[0:1] for side in sides], axis=0)
    basis_last = jnp.concatenate([side[m - 1 : m] for side in sides], axis=0)
    edge_weights[...] = jnp.concatenate(
        [
            share(basis[:, 0:m], 0, 1, here[0:1]),
            share(basis[:, last:], last, 1, here[n - 1 :]),
            share(basis_first, 0, m, turned[0:1]),
            share(basis_last, m - 1, m, turned[m - 1 :]),
        ],
        axis=1,
    )
    cells = 3 * 128
    for begin in range(0, n * m, cells):
        b0, b1, b2 = split(basis[:, begin : begin + cells])
        stacked = jnp.concatenate([b0, b0, b0, b1, b1, b2], axis=0)
        left[begin : begin + cells] = stacked.T.astype(jnp.bfloat16)


def restrict_kernel(
    partial, edge_weights, row_far, col_far, row_near, col_near, restrict, permuted, out
):
    even_x = lax.rem(lax.axis_index("sx"), 2) == 0
    even_y = lax.rem(lax.axis_index("sy"), 2) == 0
    row_low = jnp.where(even_x, row_far[...], row_near[...])
    row_high = jnp.where(even_x, row_near[...], row_far[...])
    col_low = jnp.where(even_y, col_far[...], col_near[...])
    col_high = jnp.where(even_y, col_near[...], col_far[...])
    halo = jnp.concatenate([row_low, row_high, col_low, col_high], axis=0)
    both = jnp.concatenate([partial[...] + dot(edge_weights[...], halo), restrict[...]], axis=0)
    height = both.shape[0]
    for member in range(out.shape[0] // height):
        out[member * height : (member + 1) * height] = both


def row_kernel(everyone, local_two, two, out):
    count = two.shape[0]
    height = count + 1
    third = out.shape[1]
    members = everyone.shape[0] // height
    values = jnp.concatenate([everyone[m * height : m * height + count] for m in range(members)], axis=0)
    two[...] = dot(local_two[...], values)
    shape = (count, everyone.shape[1])
    own = lax.broadcasted_iota(jnp.int32, shape, 1) // third == lax.broadcasted_iota(jnp.int32, shape, 0)
    spread = jnp.concatenate(
        [
            jnp.where(own, jnp.broadcast_to(everyone[m * height + count : (m + 1) * height], shape), 0.0)
            for m in range(members)
        ],
        axis=0,
    )
    products = dot(spread, values, ((0,), (0,)))
    terms = products[0:third]
    for k in range(1, count):
        terms = terms + products[k * third : (k + 1) * third]
    for member in range(out.shape[0]):
        out[member] = terms


def split(values):
    high = values.astype(jnp.bfloat16).astype(f32)
    rest = values - high
    mid = rest.astype(jnp.bfloat16).astype(f32)
    return high, mid, rest - mid


def correct_kernel(terms, level_three, restrict, two, left, first, result, held, sem):
    members, height, lanes = terms.shape
    placed = jnp.concatenate([terms[member] for member in range(members)], axis=0)
    three = dot(level_three[...], placed)
    coarse = two[...] + dot(restrict[...], three)
    c0, c1, c2 = split(coarse)
    right = jnp.concatenate([c0, c1, c2, c0, c1, c0], axis=0).astype(jnp.bfloat16)
    pieces = sem.shape[0]
    cells = held.shape[0] // pieces
    copies = []
    for piece in range(pieces):
        at = pl.ds(piece * cells, cells)
        held[at] = first[at] + jnp.dot(left[at], right, preferred_element_type=f32)
        copy = pltpu.make_async_copy(held.at[at], result.at[at], sem.at[piece])
        copy.start()
        copies.append(copy)
    for copy in copies:
        copy.wait()


def vmem_call(body, out_shape, inputs, name, scalars=0, scratch=()):
    whole = pl.BlockSpec(memory_space=pltpu.VMEM)
    return pl.pallas_call(
        body,
        out_shape=out_shape,
        in_specs=[pl.BlockSpec(memory_space=pltpu.SMEM)] * scalars + [whole] * (len(inputs) - scalars),
        out_specs=jax.tree.map(lambda _: whole, out_shape),
        scratch_shapes=scratch,
        compiler_params=pltpu.CompilerParams(vmem_limit_bytes=VMEM_LIMIT),
        name=name,
    )(*inputs)


def shards(
    residual,
    labels,
    region_kappa,
    coarse_basis,
    primal_cells,
    level_two,
    row_restrict,
    level_three,
    row_order,
):
    cells_x, cells_y, rhs_count = residual.shape
    coarse_count = coarse_basis.shape[0]
    cell_count = cells_x * cells_y
    local_two = level_two[0]
    local_restrict = row_restrict[0]
    coarse_third = local_restrict.shape[1]
    members_x, members_y = lax.axis_size("sx"), lax.axis_size("sy")

    zs, rhs, row_far, col_far, row_near, col_near, kap = solve(residual, labels, region_kappa)

    def swapped(edge, axis, begin):
        count = lax.axis_size(axis)
        pairs = [(i, i + 1) for i in range(begin, count - 1, 2)]
        return lax.ppermute(edge, axis, pairs + [(target, source) for source, target in pairs])

    row_far = swapped(row_far, "sx", 1)
    col_far = swapped(col_far, "sy", 1)
    row_near = swapped(row_near, "sx", 0)
    col_near = swapped(col_near, "sy", 0)

    primal = primal_cells.reshape(-1)
    basis_cells = coarse_basis.reshape(coarse_count, cell_count)
    partial, edge_weights, first, left = vmem_call(
        inner_kernel,
        (
            jax.ShapeDtypeStruct((coarse_count, rhs_count), f32),
            jax.ShapeDtypeStruct((coarse_count, 2 * (cells_x + cells_y)), f32),
            jax.ShapeDtypeStruct((cell_count, rhs_count), f32),
            jax.ShapeDtypeStruct((cell_count, 6 * coarse_count), jnp.bfloat16),
        ),
        (primal, zs, rhs, basis_cells, coarse_basis, kap),
        "inner",
        scalars=1,
        scratch=(pltpu.VMEM((cell_count, rhs_count), f32),),
    )
    order_table = (
        row_order[None, :] == jnp.arange(row_order.shape[0], dtype=jnp.int32)[:, None]
    ).astype(f32)
    permuted = jnp.dot(level_three, order_table, precision=highest)

    copies = vmem_call(
        restrict_kernel,
        jax.ShapeDtypeStruct((members_y * (coarse_count + 1), rhs_count), f32),
        (
            partial,
            edge_weights,
            row_far,
            col_far,
            row_near,
            col_near,
            local_restrict.reshape(1, coarse_count * coarse_third),
            permuted,
        ),
        "restrict",
    )
    everyone = lax.all_to_all(copies[:, None], "sy", 0, 0, tiled=True)[:, 0]
    two, copies = vmem_call(
        row_kernel,
        (
            jax.ShapeDtypeStruct((coarse_count, rhs_count), f32),
            jax.ShapeDtypeStruct((members_x, coarse_third, rhs_count), f32),
        ),
        (everyone, local_two),
        "row",
    )
    terms = lax.all_to_all(copies, "sx", 0, 0, tiled=True)

    whole = pl.BlockSpec(memory_space=pltpu.VMEM)
    result = pl.pallas_call(
        correct_kernel,
        out_shape=jax.ShapeDtypeStruct((cell_count, rhs_count), f32),
        in_specs=[whole] * 6,
        out_specs=pl.BlockSpec(memory_space=pl.ANY),
        scratch_shapes=[pltpu.VMEM((cell_count, rhs_count), f32), pltpu.SemaphoreType.DMA((6,))],
        compiler_params=pltpu.CompilerParams(vmem_limit_bytes=VMEM_LIMIT),
        name="correct",
    )(terms, permuted, local_restrict, two, left, first)
    return result.reshape(cells_x, cells_y, rhs_count)


def solution(mesh):
    in_specs = (
        P("sx", "sy", None),
        P("sx", "sy"),
        P(),
        P(None, "sx", "sy"),
        P("sx", "sy", None),
        P("sx", "sy", None),
        P("sx", "sy", None),
        P("sx", None),
        P(),
    )
    out_specs = P("sx", "sy", None)
    return jax.shard_map(shards, mesh=mesh, in_specs=in_specs, out_specs=out_specs, check_vma=False)
```

```python
import jax
import jax.numpy as jnp
from jax import lax
from jax.experimental import pallas as pl
from jax.experimental.pallas import tpu as pltpu
from jax.sharding import PartitionSpec as P

CHEB = 6


shift_mass = 1.0
lower_edge = 1.0
upper_edge = 144.0
highest = lax.Precision.HIGHEST
f32 = jnp.float32
VMEM_LIMIT = 20 * 1024 * 1024


def sweep_factors():
    centre = 0.5 * (upper_edge + lower_edge)
    half_range = 0.5 * (upper_edge - lower_edge)
    sigma_ratio = centre / half_range
    rho_now = 1.0 / sigma_ratio
    factors = []
    for sweep_index in range(CHEB):
        rho_next = 1.0 / (2.0 * sigma_ratio - rho_now)
        factors.append((rho_next * rho_now, 2.0 * rho_next / half_range))
        rho_now = rho_next
    return 1.0 / centre, factors


def dot(a, b, dims=((1,), (0,))):
    return lax.dot_general(a, b, (dims, ((), ())), precision=highest, preferred_element_type=f32)


def neighbours(source, coef_row, i, before, here_row):
    m = coef_row.shape[0]
    after = source[i + 2, 8 : 8 + m]
    beside = (before + after) + (source[i + 1, 7 : 7 + m] + source[i + 1, 9 : 9 + m])
    return after, coef_row * (beside - (4.0 + shift_mass) * here_row)


def solve_kernel(
    kappa_hbm,
    labels,
    residual,
    zs,
    rhs_out,
    row_far,
    col_far,
    col_near,
    row_near,
    kap_out,
    wide,
    rhs,
    coef,
    loaded,
    kinds,
    kappa,
    load_sem,
):
    n, m = labels.shape
    parts = load_sem.shape[0] - 2
    rows = n // parts
    kinds_copy = pltpu.make_async_copy(labels, kinds, load_sem.at[parts])
    kinds_copy.start()
    kappa_copy = pltpu.make_async_copy(kappa_hbm, kappa, load_sem.at[parts + 1])
    kappa_copy.start()
    loads = [
        pltpu.make_async_copy(
            residual.at[pl.ds(p * rows, rows)], loaded.at[pl.ds(p * rows, rows)], load_sem.at[p]
        )
        for p in range(parts)
    ]
    for copy in loads:
        copy.start()
    scale, factors = sweep_factors()
    lanes = residual.shape[2]
    zero_row = jnp.zeros((8, lanes), f32)
    for buffer in (rhs, zs):
        buffer[0] = jnp.zeros(zs.shape[1:], f32)
        buffer[n + 1] = jnp.zeros(zs.shape[1:], f32)
        for i in range(1, n + 1):
            buffer[i, 0:8] = zero_row
            buffer[i, 8 + m :] = zero_row

    kinds_copy.wait()
    kappa_copy.wait()
    here = kinds[...]
    kap = jnp.full(here.shape, kappa[0], f32)
    for region in range(1, kappa.shape[0]):
        kap = jnp.where(here == region, kappa[region], kap)
    kap_out[...] = kap
    kap_t = kap.T
    for i in range(n):
        if i % rows == 0:
            loads[i // rows].wait()
        spread = jnp.broadcast_to(kap_t[:, i : i + 1], (m, lanes))
        coef[i] = spread
        scaled = (spread * lax.rsqrt(spread)) * loaded[i]
        rhs[i + 1, 8 : 8 + m] = scaled
        rhs_out[i] = scaled

    unroll = 4
    for sweep, (keep, add) in enumerate(factors):

        def some_rows(block, carry, sweep=sweep, keep=keep, add=add):
            before, here_row = carry
            for step in range(unroll):
                i = block * unroll + step
                if sweep == 0:
                    after, product = neighbours(rhs, coef[i], i, before, here_row)
                    moved = (keep * scale + add) * here_row + (add * scale) * product
                    zs[i + 1, 8 : 8 + m] = scale * here_row + moved
                else:
                    after, product = neighbours(zs, coef[i], i, before, here_row)
                    moved = keep * wide[i] + add * (rhs_out[i] + product)
                    zs[i + 1, 8 : 8 + m] = here_row + moved
                wide[i] = moved
                before, here_row = here_row, after
            return before, here_row

        source = rhs if sweep == 0 else zs
        lax.fori_loop(0, n // unroll, some_rows, (jnp.zeros((m, lanes), f32), source[1, 8 : 8 + m]))

    even_x = lax.rem(lax.axis_index("sx"), 2) == 0
    even_y = lax.rem(lax.axis_index("sy"), 2) == 0
    row_first, row_last = zs[1, 8 : 8 + m], zs[n, 8 : 8 + m]
    row_far[...] = jnp.where(even_x, row_first, row_last)
    row_near[...] = jnp.where(even_x, row_last, row_first)
    for i in range(n):
        col_far[i : i + 1] = zs[i + 1, 8:9]
        col_near[i : i + 1] = zs[i + 1, 7 + m : 8 + m]
    col_first, col_last = col_far[...], col_near[...]
    col_far[...] = jnp.where(even_y, col_first, col_last)
    col_near[...] = jnp.where(even_y, col_last, col_first)


def solve(residual, labels, region_kappa):
    n, m, lanes = residual.shape
    field = jax.ShapeDtypeStruct((n, m, lanes), f32)
    framed = jax.ShapeDtypeStruct((n + 2, m + 16, lanes), f32)
    edge_x = jax.ShapeDtypeStruct((m, lanes), f32)
    edge_y = jax.ShapeDtypeStruct((n, lanes), f32)
    whole = pl.BlockSpec(memory_space=pltpu.VMEM)
    return pl.pallas_call(
        solve_kernel,
        out_shape=(framed, field, edge_x, edge_y, edge_y, edge_x, jax.ShapeDtypeStruct((n, m), f32)),
        in_specs=[
            pl.BlockSpec(memory_space=pltpu.HBM),
            pl.BlockSpec(memory_space=pltpu.HBM),
            pl.BlockSpec(memory_space=pltpu.HBM),
        ],
        out_specs=[whole] * 7,
        scratch_shapes=[
            pltpu.VMEM((n, m, lanes), f32),
            pltpu.VMEM((n + 2, m + 16, lanes), f32),
            pltpu.VMEM((n, m, lanes), f32),
            pltpu.VMEM((n, m, lanes), f32),
            pltpu.VMEM((n, m), jnp.int32),
            pltpu.SMEM(region_kappa.shape, f32),
            pltpu.SemaphoreType.DMA((6,)),
        ],
        compiler_params=pltpu.CompilerParams(vmem_limit_bytes=VMEM_LIMIT),
        cost_estimate=pl.CostEstimate(
            flops=80 * n * m * lanes, bytes_accessed=12 * n * m * lanes, transcendentals=0
        ),
        name="solve",
    )(
        pltpu.with_memory_space_constraint(region_kappa, pltpu.HBM),
        pltpu.with_memory_space_constraint(labels, pltpu.HBM),
        pltpu.with_memory_space_constraint(residual, pltpu.HBM),
    )


def chosen_cells(primal, width):
    function = lax.broadcasted_iota(jnp.int32, (primal.shape[0], width), 0)
    cells = jnp.full(function.shape, primal[0], jnp.int32)
    for k in range(1, primal.shape[0]):
        cells = jnp.where(function == k, primal[k], cells)
    return cells


def inner_kernel(
    primal, zs, rhs, basis, fields, kap, out, edge_weights, first, left, slack
):
    n, m, lanes = rhs.shape
    kap_t = kap[...].T
    before, here_row = jnp.zeros((m, lanes), f32), zs[1, 8 : 8 + m]
    for i in range(n):
        spread = jnp.broadcast_to(kap_t[:, i : i + 1], (m, lanes))
        after, product = neighbours(zs, spread, i, before, here_row)
        inv = lax.rsqrt(spread)
        slack[i * m : (i + 1) * m] = (rhs[i] + product) * inv
        first[i * m : (i + 1) * m] = here_row * inv
        before, here_row = here_row, after
    cell = lax.broadcasted_iota(jnp.int32, basis.shape, 1)
    weights = basis[...] + jnp.where(cell == chosen_cells(primal, basis.shape[1]), 1.0, 0.0)
    out[...] = dot(weights, slack[...])

    here = jnp.sqrt(kap[...])
    turned = here.T
    last = (n - 1) * m

    def share(weights, begin, stride, scale):
        cell = begin + stride * lax.broadcasted_iota(jnp.int32, weights.shape, 1)
        chosen = jnp.where(cell == chosen_cells(primal, weights.shape[1]), 1.0, 0.0)
        return (weights + chosen) * scale

    sides = [fields[k].T for k in range(fields.shape[0])]
    basis_first = jnp.concatenate([side[0:1] for side in sides], axis=0)
    basis_last = jnp.concatenate([side[m - 1 : m] for side in sides], axis=0)
    edge_weights[...] = jnp.concatenate(
        [
            share(basis[:, 0:m], 0, 1, here[0:1]),
            share(basis[:, last:], last, 1, here[n - 1 :]),
            share(basis_first, 0, m, turned[0:1]),
            share(basis_last, m - 1, m, turned[m - 1 :]),
        ],
        axis=1,
    )
    cells = 3 * 128
    for begin in range(0, n * m, cells):
        b0, b1, b2 = split(basis[:, begin : begin + cells])
        stacked = jnp.concatenate([b0, b0, b0, b1, b1, b2], axis=0)
        left[begin : begin + cells] = stacked.T.astype(jnp.bfloat16)


def restrict_kernel(
    partial, edge_weights, row_far, col_far, col_near, row_near, restrict, permuted, out
):
    even_x = lax.rem(lax.axis_index("sx"), 2) == 0
    even_y = lax.rem(lax.axis_index("sy"), 2) == 0
    row_low = jnp.where(even_x, row_far[...], row_near[...])
    row_high = jnp.where(even_x, row_near[...], row_far[...])
    col_low = jnp.where(even_y, col_far[...], col_near[...])
    col_high = jnp.where(even_y, col_near[...], col_far[...])
    halo = jnp.concatenate([row_low, row_high, col_low, col_high], axis=0)
    both = jnp.concatenate([partial[...] + dot(edge_weights[...], halo), restrict[...]], axis=0)
    height = both.shape[0]
    for member in range(out.shape[0] // height):
        out[member * height : (member + 1) * height] = both


def row_kernel(everyone, local_two, two, out):
    count = two.shape[0]
    height = count + 1
    third = out.shape[1]
    members = everyone.shape[0] // height
    values = jnp.concatenate([everyone[m * height : m * height + count] for m in range(members)], axis=0)
    two[...] = dot(local_two[...], values)
    shape = (count, everyone.shape[1])
    own = lax.broadcasted_iota(jnp.int32, shape, 1) // third == lax.broadcasted_iota(jnp.int32, shape, 0)
    spread = jnp.concatenate(
        [
            jnp.where(own, jnp.broadcast_to(everyone[m * height + count : (m + 1) * height], shape), 0.0)
            for m in range(members)
        ],
        axis=0,
    )
    products = dot(spread, values, ((0,), (0,)))
    terms = products[0:third]
    for k in range(1, count):
        terms = terms + products[k * third : (k + 1) * third]
    for member in range(out.shape[0]):
        out[member] = terms


def split(values):
    high = values.astype(jnp.bfloat16).astype(f32)
    rest = values - high
    mid = rest.astype(jnp.bfloat16).astype(f32)
    return high, mid, rest - mid


def correct_kernel(terms, level_three, restrict, two, left, first, result, held, sem):
    members, height, lanes = terms.shape
    placed = jnp.concatenate([terms[member] for member in range(members)], axis=0)
    three = dot(level_three[...], placed)
    coarse = two[...] + dot(restrict[...], three)
    c0, c1, c2 = split(coarse)
    right = jnp.concatenate([c0, c1, c2, c0, c1, c0], axis=0).astype(jnp.bfloat16)
    pieces = sem.shape[0]
    cells = held.shape[0] // pieces
    copies = []
    for piece in range(pieces):
        at = pl.ds(piece * cells, cells)
        held[at] = first[at] + jnp.dot(left[at], right, preferred_element_type=f32)
        copy = pltpu.make_async_copy(held.at[at], result.at[at], sem.at[piece])
        copy.start()
        copies.append(copy)
    for copy in copies:
        copy.wait()


def vmem_call(body, out_shape, inputs, name, scalars=0, scratch=()):
    whole = pl.BlockSpec(memory_space=pltpu.VMEM)
    return pl.pallas_call(
        body,
        out_shape=out_shape,
        in_specs=[pl.BlockSpec(memory_space=pltpu.SMEM)] * scalars + [whole] * (len(inputs) - scalars),
        out_specs=jax.tree.map(lambda _: whole, out_shape),
        scratch_shapes=scratch,
        compiler_params=pltpu.CompilerParams(vmem_limit_bytes=VMEM_LIMIT),
        name=name,
    )(*inputs)


def shards(
    residual,
    labels,
    region_kappa,
    coarse_basis,
    primal_cells,
    level_two,
    row_restrict,
    level_three,
    row_order,
):
    cells_x, cells_y, rhs_count = residual.shape
    coarse_count = coarse_basis.shape[0]
    cell_count = cells_x * cells_y
    local_two = level_two[0]
    local_restrict = row_restrict[0]
    coarse_third = local_restrict.shape[1]
    members_x, members_y = lax.axis_size("sx"), lax.axis_size("sy")

    zs, rhs, row_far, col_far, col_near, row_near, kap = solve(residual, labels, region_kappa)

    def swapped(edge, axis, begin):
        count = lax.axis_size(axis)
        pairs = [(i, i + 1) for i in range(begin, count - 1, 2)]
        return lax.ppermute(edge, axis, pairs + [(target, source) for source, target in pairs])

    row_far = swapped(row_far, "sx", 1)
    col_far = swapped(col_far, "sy", 1)
    col_near = swapped(col_near, "sy", 0)
    row_near = swapped(row_near, "sx", 0)

    primal = primal_cells.reshape(-1)
    basis_cells = coarse_basis.reshape(coarse_count, cell_count)
    partial, edge_weights, first, left = vmem_call(
        inner_kernel,
        (
            jax.ShapeDtypeStruct((coarse_count, rhs_count), f32),
            jax.ShapeDtypeStruct((coarse_count, 2 * (cells_x + cells_y)), f32),
            jax.ShapeDtypeStruct((cell_count, rhs_count), f32),
            jax.ShapeDtypeStruct((cell_count, 6 * coarse_count), jnp.bfloat16),
        ),
        (primal, zs, rhs, basis_cells, coarse_basis, kap),
        "inner",
        scalars=1,
        scratch=(pltpu.VMEM((cell_count, rhs_count), f32),),
    )
    order_table = (
        row_order[None, :] == jnp.arange(row_order.shape[0], dtype=jnp.int32)[:, None]
    ).astype(f32)
    permuted = jnp.dot(level_three, order_table, precision=highest)

    copies = vmem_call(
        restrict_kernel,
        jax.ShapeDtypeStruct((members_y * (coarse_count + 1), rhs_count), f32),
        (
            partial,
            edge_weights,
            row_far,
            col_far,
            col_near,
            row_near,
            local_restrict.reshape(1, coarse_count * coarse_third),
            permuted,
        ),
        "restrict",
    )
    everyone = lax.all_to_all(copies[:, None], "sy", 0, 0, tiled=True)[:, 0]
    two, copies = vmem_call(
        row_kernel,
        (
            jax.ShapeDtypeStruct((coarse_count, rhs_count), f32),
            jax.ShapeDtypeStruct((members_x, coarse_third, rhs_count), f32),
        ),
        (everyone, local_two),
        "row",
    )
    terms = lax.all_to_all(copies, "sx", 0, 0, tiled=True)

    whole = pl.BlockSpec(memory_space=pltpu.VMEM)
    result = pl.pallas_call(
        correct_kernel,
        out_shape=jax.ShapeDtypeStruct((cell_count, rhs_count), f32),
        in_specs=[whole] * 6,
        out_specs=pl.BlockSpec(memory_space=pl.ANY),
        scratch_shapes=[pltpu.VMEM((cell_count, rhs_count), f32), pltpu.SemaphoreType.DMA((6,))],
        compiler_params=pltpu.CompilerParams(vmem_limit_bytes=VMEM_LIMIT),
        name="correct",
    )(terms, permuted, local_restrict, two, left, first)
    return result.reshape(cells_x, cells_y, rhs_count)


def solution(mesh):
    in_specs = (
        P("sx", "sy", None),
        P("sx", "sy"),
        P(),
        P(None, "sx", "sy"),
        P("sx", "sy", None),
        P("sx", "sy", None),
        P("sx", "sy", None),
        P("sx", None),
        P(),
    )
    out_specs = P("sx", "sy", None)
    return jax.shard_map(shards, mesh=mesh, in_specs=in_specs, out_specs=out_specs, check_vma=False)
```
